32 devices in a mesh: inner: 4 (over x, core), outer: 8 (over z, y).
Axes of the slice: x: 2, y: 2, z: 4, core: 2. Of those that a mesh axis runs over, the one named last changes fastest.
Arguments:
- frames: bfloat16 [4096, 512], P(('inner', 'outer')), as said below
- attention_gain: float32 [512], replicated, may hold values from 0.5 to 1.5
- qkv_weight: bfloat16 [512, 1536], replicated
- out_weight: bfloat16 [512, 512], replicated, may hold values from -0.25 to 0.25
- head_gain: float32 [512], replicated, may hold values from 0.5 to 1.5
- head_weight: bfloat16 [512, 1024], replicated
- frame_valid: int32 [4096], P(('inner', 'outer')), may hold values 0 or 1
- targets: int32 [4096], P(('inner', 'outer')), may hold values from 0 to 1023
Outputs:
- grad_input: float32 [4096, 512], P(('inner', 'outer'))
- grad_qkv: float32 [512, 1536], P('outer', 'inner')
- grad_out: float32 [512, 512], P('outer', 'inner')
The draws below stay inside these ranges and needn't reach their ends.
Inputs may be any that keep to these rules, and one draw needn't show every extreme that they name: Input frames.
All inputs are finite; a program needn't handle non-finite values. No bound on the sum of `frame_valid` on one device may be relied on, other than what follows from the above.
Results may differ from the reference program's by a relative error of at most 0.015.
Values may be sent and summed in bfloat16 or wider, within the bound.
No kernel may reach another device: no remote copies, remote signals or barrier semaphores. Data moves between devices by JAX's collectives and lax.ppermute only.
A program may use at most 64 MiB of HBM per device.

```python
import math
import jax
import jax.numpy as jnp
from jax import lax

D = 512
HEADS = 8
CODES = 1024
WIN = 128
TOK_DEV = 128
TOKENS = 4096


def draw_frames(key, part):
    base = jax.random.normal(jax.random.fold_in(key, 11), (TOKENS, D), jnp.float32)
    return base.astype(jnp.bfloat16)


def draw_qkv_weight(key, part):
    blocks = jax.random.normal(jax.random.fold_in(key, 21), (3, D, D), jnp.float32) * (1.0 / math.sqrt(D))
    query_part = blocks[0]
    key_part = blocks[1]
    value_part = blocks[2]
    return jnp.concatenate([query_part, key_part, value_part], 1).astype(jnp.bfloat16)


def draw_head_weight(key, part):
    base = jax.random.normal(jax.random.fold_in(key, 31), (D, CODES), jnp.float32) * (3.0 / math.sqrt(D))
    return base.astype(jnp.bfloat16)


def plant(values, rng, low, high):
    place = [jax.random.randint(jax.random.fold_in(rng, axis), (), 0, length) for axis, length in enumerate(values.shape)]
    widest = values.shape.index(max(values.shape))
    beside = place[:widest] + [(place[widest] + 1) % values.shape[widest]] + place[widest + 1:]
    return values.at[tuple(place)].set(low).at[tuple(beside)].set(high)


def noise(own_key, extent, width, limit, held_as=jnp.bfloat16):
    return jnp.clip(width * jax.random.normal(own_key, extent, jnp.float32), -limit, limit).astype(held_as)


def setup_inputs(seed: int = 0) -> dict:
    arg_keys = jax.random.split(jax.random.key(seed), 9)
    frames = draw_frames(jax.random.fold_in(arg_keys[8], 71), 0)
    attention_gain = jnp.clip(1.0 + 0.1 * jax.random.normal(arg_keys[1], (D,), jnp.float32), 0.5, 1.5)
    qkv_weight = draw_qkv_weight(jax.random.fold_in(arg_keys[8], 71), 0)
    out_weight = noise(arg_keys[3], (D, D), D ** -0.5, 0.25)
    head_gain = jnp.clip(1.0 + 0.1 * jax.random.normal(arg_keys[4], (D,), jnp.float32), 0.5, 1.5)
    head_weight = draw_head_weight(jax.random.fold_in(arg_keys[8], 71), 0)
    frame_valid = plant((jax.random.randint(arg_keys[6], (TOKENS,), 0, 4) < 3).astype(jnp.int32), jax.random.fold_in(arg_keys[6], 1), 0, 1)
    targets = plant(jax.random.randint(arg_keys[7], (TOKENS,), 0, CODES), jax.random.fold_in(arg_keys[7], 1), 0, CODES - 1).astype(jnp.int32)
    return {"frames": frames, "attention_gain": attention_gain, "qkv_weight": qkv_weight, "out_weight": out_weight, "head_gain": head_gain, "head_weight": head_weight, "frame_valid": frame_valid, "targets": targets}


def layer_norm(source, norm_gain):
    row_mean = lax.optimization_barrier(jnp.mean(source, axis=-1, keepdims=True))
    centred = source - row_mean
    variance = lax.optimization_barrier(jnp.mean(centred * centred, axis=-1, keepdims=True))
    inverse = lax.rsqrt(variance + 1e-05)
    normed = centred * inverse
    return (normed * norm_gain, normed, inverse)

def norm_back(upstream, normed, inverse, norm_gain):
    scaled = upstream * norm_gain
    return inverse * (scaled - lax.optimization_barrier(jnp.mean(scaled, axis=-1, keepdims=True)) - normed * lax.optimization_barrier(jnp.mean(scaled * normed, axis=-1, keepdims=True)))

def band_probs(queries, key_rows, first_row, total_rows):
    query_count = queries.shape[0]
    key_count = key_rows.shape[0]
    head_size = queries.shape[1] // HEADS
    query_heads = queries.reshape(query_count, HEADS, head_size).astype(jnp.float32)
    key_heads = key_rows.reshape(key_count, HEADS, head_size).astype(jnp.float32)
    scores = jnp.einsum('thd,uhd->htu', query_heads, key_heads) * (1.0 / math.sqrt(head_size))
    query_pos = lax.broadcasted_iota(jnp.int32, (query_count, key_count), 0)
    key_pos = lax.broadcasted_iota(jnp.int32, (query_count, key_count), 1)
    distance = key_pos - WIN - query_pos
    key_global = first_row - WIN + key_pos
    allowed = (jnp.abs(distance) <= WIN) & (key_global >= 0) & (key_global < total_rows)
    scores = jnp.where(allowed[None], scores, jnp.float32(-1e+30))
    row_max = lax.optimization_barrier(jnp.max(scores, axis=-1, keepdims=True))
    weights = jnp.exp(scores - row_max)
    return weights / lax.optimization_barrier(jnp.sum(weights, axis=-1, keepdims=True))

def attend(queries, pair_rows, first_row, total_rows):
    features = queries.shape[1]
    weights = band_probs(queries, pair_rows[:, :features], first_row, total_rows)
    weights_low = weights.astype(jnp.bfloat16)
    value_heads = pair_rows[:, features:].reshape(pair_rows.shape[0], HEADS, -1).astype(jnp.float32)
    combined = jnp.einsum('htu,uhd->thd', weights_low.astype(jnp.float32), value_heads)
    return combined.reshape(queries.shape[0], features).astype(jnp.bfloat16)

def attend_back(queries, pair_rows, grad_attended, first_row, total_rows):
    query_count, features = queries.shape
    key_count = pair_rows.shape[0]
    head_size = features // HEADS
    weights = band_probs(queries, pair_rows[:, :features], first_row, total_rows)
    weights_low = weights.astype(jnp.bfloat16).astype(jnp.float32)
    query_heads = queries.reshape(query_count, HEADS, head_size).astype(jnp.float32)
    key_heads = pair_rows[:, :features].reshape(key_count, HEADS, head_size).astype(jnp.float32)
    value_heads = pair_rows[:, features:].reshape(key_count, HEADS, head_size).astype(jnp.float32)
    grad_heads = grad_attended.reshape(query_count, HEADS, head_size).astype(jnp.float32)
    grad_weights = jnp.einsum('thd,uhd->htu', grad_heads, value_heads)
    row_dot = lax.optimization_barrier(jnp.sum(weights * grad_weights, axis=-1, keepdims=True))
    grad_scores = (weights * (grad_weights - row_dot) * (1.0 / math.sqrt(head_size))).astype(jnp.bfloat16).astype(jnp.float32)
    grad_query = jnp.einsum('htu,uhd->thd', grad_scores, key_heads).reshape(query_count, features).astype(jnp.bfloat16)
    grad_keys = jnp.einsum('htu,thd->uhd', grad_scores, query_heads).reshape(key_count, features)
    grad_values = jnp.einsum('htu,thd->uhd', weights_low, grad_heads).reshape(key_count, features)
    return (grad_query, jnp.concatenate([grad_keys, grad_values], 1))

def reference(frames, attention_gain, qkv_weight, out_weight, head_gain, head_weight, frame_valid, targets):
    source = frames.astype(jnp.float32)
    features = source.shape[1]
    attn_normed, attn_hat, attn_inverse = layer_norm(source, attention_gain)
    normed_in = attn_normed.astype(jnp.bfloat16)
    projected = jnp.dot(normed_in, qkv_weight, preferred_element_type=jnp.float32).astype(jnp.bfloat16)
    queries = projected[:, :features]
    padded = jnp.pad(projected[:, features:], ((WIN, WIN), (0, 0)))
    block_count = TOKENS // TOK_DEV
    starts = jnp.arange(block_count, dtype=jnp.int32) * TOK_DEV

    def forward_block(offset):
        query_block = lax.dynamic_slice_in_dim(queries, offset, TOK_DEV, 0)
        pair_block = lax.dynamic_slice_in_dim(padded, offset, TOK_DEV + 2 * WIN, 0)
        return attend(query_block, pair_block, offset, TOKENS)
    attended = lax.map(forward_block, starts).reshape(TOKENS, features)
    residual = (source + jnp.dot(attended, out_weight, preferred_element_type=jnp.float32)).astype(jnp.bfloat16)
    head_normed, head_hat, head_inverse = layer_norm(residual.astype(jnp.float32), head_gain)
    head_in = head_normed.astype(jnp.bfloat16)

    def head_block(offset):
        row_block = lax.dynamic_slice_in_dim(head_in, offset, TOK_DEV, 0)
        labels = lax.dynamic_slice_in_dim(targets, offset, TOK_DEV, 0)
        valid_block = lax.dynamic_slice_in_dim(frame_valid, offset, TOK_DEV, 0)
        logits = jnp.dot(row_block, head_weight, preferred_element_type=jnp.float32)
        predicted = jax.nn.softmax(logits, axis=-1)
        one_hot = (labels[:, None] == lax.broadcasted_iota(jnp.int32, (TOK_DEV, CODES), 1)).astype(jnp.float32)
        grad_logits = (valid_block[:, None].astype(jnp.float32) * (predicted - one_hot)).astype(jnp.bfloat16)
        return lax.dot_general(grad_logits, head_weight, (((1,), (1,)), ((), ())), preferred_element_type=jnp.float32)
    grad_head = lax.map(head_block, starts).reshape(TOKENS, features)
    grad_resid = norm_back(grad_head, head_hat, head_inverse, head_gain)
    resid_low = grad_resid.astype(jnp.bfloat16)
    grad_out = lax.dot_general(attended, resid_low, (((0,), (0,)), ((), ())), preferred_element_type=jnp.float32)
    grad_attended = lax.dot_general(resid_low, out_weight, (((1,), (1,)), ((), ())), preferred_element_type=jnp.float32).astype(jnp.bfloat16)

    def backward_block(key_grads, offset):
        query_block = lax.dynamic_slice_in_dim(queries, offset, TOK_DEV, 0)
        pair_block = lax.dynamic_slice_in_dim(padded, offset, TOK_DEV + 2 * WIN, 0)
        grad_block = lax.dynamic_slice_in_dim(grad_attended, offset, TOK_DEV, 0)
        grad_query, grad_pairs = attend_back(query_block, pair_block, grad_block, offset, TOKENS)
        current = lax.dynamic_slice_in_dim(key_grads, offset, TOK_DEV + 2 * WIN, 0)
        key_grads = lax.dynamic_update_slice_in_dim(key_grads, current + grad_pairs, offset, 0)
        return (key_grads, grad_query)
    initial = jnp.zeros((TOKENS + 2 * WIN, 2 * features), jnp.float32)
    key_grads, grad_queries = lax.scan(backward_block, initial, starts)
    grad_proj = jnp.concatenate([grad_queries.reshape(TOKENS, features), key_grads[WIN:WIN + TOKENS].astype(jnp.bfloat16)], 1)
    grad_qkv = lax.dot_general(normed_in, grad_proj, (((0,), (0,)), ((), ())), preferred_element_type=jnp.float32)
    grad_normed = lax.dot_general(grad_proj, qkv_weight, (((1,), (1,)), ((), ())), preferred_element_type=jnp.float32)
    grad_input = grad_resid + norm_back(grad_normed, attn_hat, attn_inverse, attention_gain)
    return (grad_input, grad_qkv, grad_out)
```

```python
import functools
import math

import jax
import jax.numpy as jnp
from jax import lax
from jax.experimental import pallas as pl
from jax.experimental.pallas import tpu as pltpu
from jax.sharding import PartitionSpec as P

HEADS = 8
WIN = 128
LANES = 128
BF = jnp.bfloat16
F32 = jnp.float32
EVERY = ("inner", "outer")


def mm(left_side, right_side):
    return jnp.dot(left_side, right_side, preferred_element_type=F32)


def mm_cols(left_side, right_side):
    return lax.dot_general(
        left_side, right_side, (((1,), (1,)), ((), ())), preferred_element_type=F32
    )


def mm_rows(left_side, right_side):
    return lax.dot_general(
        left_side, right_side, (((0,), (0,)), ((), ())), preferred_element_type=F32
    )


def normalize(source):
    centred = source - jnp.mean(source, axis=-1, keepdims=True)
    variance = jnp.mean(centred * centred, axis=-1, keepdims=True)
    inverse = lax.rsqrt(variance + 1e-05)
    return centred * inverse, inverse


def norm_back(upstream, normed, inverse, norm_gain):
    scaled = upstream * norm_gain
    return inverse * (
        scaled
        - jnp.mean(scaled, axis=-1, keepdims=True)
        - normed * jnp.mean(scaled * normed, axis=-1, keepdims=True)
    )


def as_column(row):
    size = row.shape[1]
    eye = lax.broadcasted_iota(jnp.int32, (size, size), 0) == lax.broadcasted_iota(
        jnp.int32, (size, size), 1
    )
    return jnp.sum(jnp.where(eye, row.astype(F32), 0.0), axis=1, keepdims=True)


def own_kernel(frames, gain, qkv_weight, normed_out, projected_out):
    hat, _ = normalize(frames[...].astype(F32))
    normed = (hat * gain[...]).astype(BF)
    normed_out[...] = normed
    projected_out[...] = mm(normed, qkv_weight[...]).astype(BF)


def spread_heads(pair, low_lanes):
    zero = jnp.zeros_like(pair)
    return jnp.concatenate([jnp.where(low_lanes, pair, zero), jnp.where(low_lanes, zero, pair)], 0)


def main_kernel(
    device_count,
    head_size,
    frames,
    halo_one,
    halo_two,
    normed,
    projected,
    gain,
    qkv_weight,
    out_weight,
    head_gain,
    head_weight,
    frame_valid,
    targets,
    normed_all,
    grad_pairs,
    attended,
    resid_low,
    grad_resid,
    grad_normed,
    send_one,
    send_two,
    pairs,
    weights,
):
    rows, features = frames.shape
    position = lax.axis_index(EVERY)
    odd = lax.rem(position, 2) == 1
    row_one = pl.multiple_of(jnp.where(odd, 0, WIN + rows), 128)
    row_two = pl.multiple_of(jnp.where(odd, WIN + rows, 0), 128)
    scale = 1.0 / math.sqrt(head_size)
    key_count = rows + 2 * WIN

    for row, halo in ((row_one, halo_one), (row_two, halo_two)):
        hat, _ = normalize(halo[...].astype(F32))
        rim = (hat * gain[...]).astype(BF)
        normed_all[pl.ds(row, WIN), :] = rim
        pairs[pl.ds(row, WIN), :] = mm(rim, qkv_weight[:, features:]).astype(BF)
    normed_all[WIN : WIN + rows, :] = normed[...]
    pairs[WIN : WIN + rows, :] = projected[:, features:]

    query_pos = lax.broadcasted_iota(jnp.int32, (rows, key_count), 0)
    key_pos = lax.broadcasted_iota(jnp.int32, (rows, key_count), 1)
    first = jnp.where(position == 0, WIN, 0)
    last = jnp.where(position == device_count - 1, WIN + rows, key_count)
    distance = key_pos - WIN - query_pos
    allowed = (jnp.abs(distance) <= WIN) & (key_pos >= first) & (key_pos < last)
    bias = jnp.where(allowed, 0.0, -1e30).astype(F32)
    bias = jnp.concatenate([bias, bias], 0)
    low_lanes = lax.broadcasted_iota(jnp.int32, (rows, LANES), 1) < head_size
    groups = features // LANES

    for g in range(groups):
        cols = slice(g * LANES, (g + 1) * LANES)
        values = slice(features + g * LANES, features + (g + 1) * LANES)
        queries = spread_heads(projected[:, cols] * BF(scale), low_lanes)
        scores = mm_cols(queries, pairs[:, cols]) + bias
        powers = jnp.exp(scores - jnp.max(scores, axis=-1, keepdims=True))
        share = powers * (1.0 / jnp.sum(powers, axis=-1, keepdims=True))
        weights[g] = share
        mixed = mm(share.astype(BF), pairs[:, values])
        attended[:, cols] = jnp.where(low_lanes, mixed[:rows], mixed[rows:]).astype(BF)

    residual = (frames[...].astype(F32) + mm(attended[...], out_weight[...])).astype(BF)
    head_hat, head_inverse = normalize(residual.astype(F32))
    head_in = (head_hat * head_gain[...]).astype(BF)
    logits = mm(head_in, head_weight[...])
    powers = jnp.exp(logits - jnp.max(logits, axis=-1, keepdims=True))
    predicted = powers * (1.0 / jnp.sum(powers, axis=-1, keepdims=True))
    codes = lax.broadcasted_iota(jnp.int32, logits.shape, 1).astype(F32)
    one_hot = jnp.where(codes == as_column(targets[...]), 1.0, 0.0)
    grad_logits = (as_column(frame_valid[...]) * (predicted - one_hot)).astype(BF)
    grad_head = mm_cols(grad_logits, head_weight[...])
    resid = norm_back(grad_head, head_hat, head_inverse, head_gain[...])
    grad_resid[...] = resid
    low = resid.astype(BF)
    resid_low[...] = low
    grad_attended = mm_cols(low, out_weight[...]).astype(BF)

    grad_pairs[0:WIN, 0:features] = jnp.zeros((WIN, features), BF)
    grad_pairs[WIN + rows :, 0:features] = jnp.zeros((WIN, features), BF)
    for g in range(groups):
        cols = slice(g * LANES, (g + 1) * LANES)
        values = slice(features + g * LANES, features + (g + 1) * LANES)
        queries = spread_heads(projected[:, cols] * BF(scale), low_lanes)
        upstream = spread_heads(grad_attended[:, cols], low_lanes)
        share = weights[g]
        grad_weights = mm_cols(upstream, pairs[:, values])
        row_dot = jnp.sum(share * grad_weights, axis=-1, keepdims=True)
        grad_scores = (share * (grad_weights - row_dot)).astype(BF)
        mixed = mm(grad_scores, pairs[:, cols])
        grad_query = jnp.where(low_lanes, mixed[:rows], mixed[rows:]) * scale
        grad_pairs[WIN : WIN + rows, cols] = grad_query.astype(BF)
        grad_pairs[:, features + g * LANES : features + (g + 1) * LANES] = mm_rows(
            grad_scores, queries
        ).astype(BF)
        grad_pairs[:, 2 * features + g * LANES : 2 * features + (g + 1) * LANES] = mm_rows(
            share.astype(BF), upstream
        ).astype(BF)

    grad_normed[...] = mm_cols(grad_pairs[WIN : WIN + rows, :], qkv_weight[...])
    send_one[...] = mm_cols(
        grad_pairs[pl.ds(row_one, WIN), features:], qkv_weight[:, features:]
    ).astype(BF)
    send_two[...] = mm_cols(
        grad_pairs[pl.ds(row_two, WIN), features:], qkv_weight[:, features:]
    ).astype(BF)


def input_kernel(frames, gain, grad_resid, grad_normed, from_one, from_two, grad_input):
    hat, inverse = normalize(frames[...].astype(F32))
    total = grad_normed[...] + from_one[...].astype(F32) + from_two[...].astype(F32)
    grad_input[...] = grad_resid[...] + norm_back(total, hat, inverse, gain[...])


def half_kernel(sizes, other, normed_all, grad_pairs, attended, resid_low, share):
    inner_count, outer_count = sizes
    features = normed_all.shape[1]
    core = lax.rem(lax.axis_index("inner"), 2)
    if other:
        core = 1 - core
    wide = grad_pairs.shape[1] // inner_count
    narrow = features // inner_count
    tall = features // outer_count
    for x in range(inner_count // 2):
        block = 2 * x + core
        left = mm_rows(
            normed_all[...], grad_pairs[:, pl.ds(pl.multiple_of(block * wide, LANES), wide)]
        ).astype(share.dtype)
        right = mm_rows(
            attended[...], resid_low[:, pl.ds(pl.multiple_of(block * narrow, LANES), narrow)]
        ).astype(share.dtype)
        for o in range(outer_count):
            z, y = divmod(o, 2)
            row = ((x * 2 + y) * (outer_count // 2) + z) * tall
            share[row : row + tall, :wide] = left[o * tall : (o + 1) * tall]
            share[row : row + tall, wide:] = right[o * tall : (o + 1) * tall]


def square_kernel(sizes, kept, received, *outs):
    inner_count, _ = sizes
    x = lax.axis_index("inner") // 2
    y = lax.rem(lax.axis_index("outer"), 2)
    parts = inner_count
    height = kept.shape[0] // parts
    mine = x * 2 + y
    for k, out in enumerate(outs):
        row = pl.multiple_of((mine ^ k) * height, height)
        total = kept[pl.ds(row, height), :] + received[pl.ds(row, height), :].astype(F32)
        out[...] = total.astype(out.dtype)


def line_kernel(sizes, kept, *refs):
    inner_count, outer_count = sizes
    received, outs = refs[: inner_count - 1], refs[inner_count - 1 :]
    parts = outer_count // 2
    height = kept.shape[0] // parts
    mine = lax.axis_index("outer") // 2
    for k, out in enumerate(outs):
        rows = pl.ds(pl.multiple_of((mine ^ k) * height, height), height)
        total = kept[rows, :]
        for other in received:
            total = total + other[rows, :].astype(F32)
        out[...] = total.astype(out.dtype)


def last_kernel(kept, *refs):
    received, (qkv_out, out_out) = refs[:-2], refs[-2:]
    total = kept[...]
    for other in received:
        total = total + other[...].astype(F32)
    wide = qkv_out.shape[1]
    qkv_out[...] = total[:, :wide]
    out_out[...] = total[:, wide:]


def full_kernel(normed_all, grad_pairs, attended, resid_low, qkv_out, out_out):
    qkv_out[...] = mm_rows(normed_all[...], grad_pairs[...])
    out_out[...] = mm_rows(attended[...], resid_low[...])


def call(kernel, outs, *args, name, scratch=()):
    shapes = [jax.ShapeDtypeStruct(shape, dtype) for shape, dtype in outs]
    spec = pl.BlockSpec(memory_space=pltpu.VMEM)
    return pl.pallas_call(
        kernel,
        out_shape=shapes,
        in_specs=[spec] * len(args),
        out_specs=[spec] * len(shapes),
        scratch_shapes=list(scratch),
        name=name,
    )(*args)


def grid_swap(sizes, inner_bits, outer_bits):
    inner_count, outer_count = sizes
    return [
        (i * outer_count + o, (i ^ inner_bits) * outer_count + (o ^ outer_bits))
        for i in range(inner_count)
        for o in range(outer_count)
    ]


def swap(value, sizes, inner_bits, outer_bits):
    return lax.ppermute(value, EVERY, grid_swap(sizes, inner_bits, outer_bits))


def neighbour_swaps(device_count):
    near = [(i, i ^ 1) for i in range(device_count // 2 * 2)]
    far = [(i, i + 1) for i in range(1, device_count - 1, 2)]
    return near, far + [(j, i) for i, j in far]


def power_of_two(count):
    return count > 1 and count & (count - 1) == 0


def per_device(
    sizes,
    frames,
    attention_gain,
    qkv_weight,
    out_weight,
    head_gain,
    head_weight,
    frame_valid,
    targets,
):
    inner_count, outer_count = sizes
    device_count = inner_count * outer_count
    rows, features = frames.shape
    columns = qkv_weight.shape[1]
    key_count = rows + 2 * WIN
    near, far = neighbour_swaps(device_count)
    halo_two = lax.ppermute(frames, EVERY, far)
    halo_one = lax.ppermute(frames, EVERY, near)
    gain = attention_gain.reshape(1, features)
    normed, projected = call(
        own_kernel,
        [((rows, features), BF), ((rows, columns), BF)],
        frames,
        gain,
        qkv_weight,
        name="own",
    )
    (
        normed_all,
        grad_pairs,
        attended,
        resid_low,
        grad_resid,
        grad_normed,
        send_one,
        send_two,
    ) = call(
        functools.partial(main_kernel, device_count, features // HEADS),
        [
            ((key_count, features), BF),
            ((key_count, columns), BF),
            ((rows, features), BF),
            ((rows, features), BF),
            ((rows, features), F32),
            ((rows, features), F32),
            ((WIN, features), BF),
            ((WIN, features), BF),
        ],
        frames,
        halo_one,
        halo_two,
        normed,
        projected,
        gain,
        qkv_weight,
        out_weight,
        head_gain.reshape(1, features),
        head_weight,
        frame_valid.reshape(1, rows),
        targets.reshape(1, rows),
        name="main",
        scratch=[
            pltpu.VMEM((key_count, 2 * features), BF),
            pltpu.VMEM((features // LANES, 2 * rows, key_count), F32),
        ],
    )
    from_two = lax.ppermute(send_two, EVERY, far)
    from_one = lax.ppermute(send_one, EVERY, near)
    (grad_input,) = call(
        input_kernel,
        [((rows, features), F32)],
        frames,
        gain,
        grad_resid,
        grad_normed,
        from_one,
        from_two,
        name="input",
    )
    terms = (normed_all, grad_pairs, attended, resid_low)
    wide, narrow = columns // inner_count, features // inner_count
    tall = features // outer_count
    tiled = wide % LANES == 0 and narrow % LANES == 0 and tall % 16 == 0
    if tiled and power_of_two(inner_count) and power_of_two(outer_count):
        half = inner_count // 2 * features
        width = wide + narrow
        (away,) = call(
            functools.partial(half_kernel, sizes, True), [((half, width), BF)], *terms, name="away"
        )
        received = swap(away, sizes, 1, 0)
        (home,) = call(
            functools.partial(half_kernel, sizes, False), [((half, width), F32)], *terms, name="home"
        )
        height = half // inner_count
        kept, *sends = call(
            functools.partial(square_kernel, sizes),
            [((height, width), F32)] + [((height, width), BF)] * (inner_count - 1),
            home,
            received,
            name="square",
        )
        got = [
            swap(send, sizes, (k >> 1) << 1, k & 1)
            for k, send in reversed(list(enumerate(sends, 1)))
        ]
        parts = outer_count // 2
        kept, *sends = call(
            functools.partial(line_kernel, sizes),
            [((tall, width), F32)] + [((tall, width), BF)] * (parts - 1),
            kept,
            *got,
            name="line",
        )
        got = [swap(send, sizes, 0, k << 1) for k, send in reversed(list(enumerate(sends, 1)))]
        grad_qkv, grad_out = call(
            last_kernel, [((tall, wide), F32), ((tall, narrow), F32)], kept, *got, name="last"
        )
        return grad_input, grad_qkv, grad_out
    proj_term, output_term = call(
        full_kernel, [((features, columns), F32), ((features, features), F32)], *terms, name="full"
    )
    proj_term = proj_term.reshape(features, inner_count, wide)
    output_term = output_term.reshape(features, inner_count, narrow)
    joined = jnp.concatenate([proj_term, output_term], 2).reshape(features, -1)
    shares = lax.psum_scatter(joined, "inner", scatter_dimension=1, tiled=True)
    shares = lax.psum_scatter(shares, "outer", scatter_dimension=0, tiled=True)
    return grad_input, shares[:, :wide], shares[:, wide:]


def solution(mesh):
    sizes = (mesh.shape["inner"], mesh.shape["outer"])
    spread = P(EVERY)
    return jax.shard_map(
        functools.partial(per_device, sizes),
        mesh=mesh,
        in_specs=(P(EVERY, None), P(), P(), P(), P(), P(), spread, spread),
        out_specs=(P(EVERY, None), P("outer", "inner"), P("outer", "inner")),
        check_vma=False,
    )
```

```python
import functools
import math

import jax
import jax.numpy as jnp
from jax import lax
from jax.experimental import pallas as pl
from jax.experimental.pallas import tpu as pltpu
from jax.sharding import PartitionSpec as P

HEADS = 8
WIN = 128
LANES = 128
BF = jnp.bfloat16
F32 = jnp.float32
EVERY = ("inner", "outer")


def mm(left_side, right_side):
    return jnp.dot(left_side, right_side, preferred_element_type=F32)


def mm_cols(left_side, right_side):
    return lax.dot_general(
        left_side, right_side, (((1,), (1,)), ((), ())), preferred_element_type=F32
    )


def mm_rows(left_side, right_side):
    return lax.dot_general(
        left_side, right_side, (((0,), (0,)), ((), ())), preferred_element_type=F32
    )


def normalize(source):
    centred = source - jnp.mean(source, axis=-1, keepdims=True)
    variance = jnp.mean(centred * centred, axis=-1, keepdims=True)
    inverse = lax.rsqrt(variance + 1e-05)
    return centred * inverse, inverse


def norm_back(upstream, normed, inverse, norm_gain):
    scaled = upstream * norm_gain
    return inverse * (
        scaled
        - jnp.mean(scaled, axis=-1, keepdims=True)
        - normed * jnp.mean(scaled * normed, axis=-1, keepdims=True)
    )


def as_column(row):
    size = row.shape[1]
    eye = lax.broadcasted_iota(jnp.int32, (size, size), 0) == lax.broadcasted_iota(
        jnp.int32, (size, size), 1
    )
    return jnp.sum(jnp.where(eye, row.astype(F32), 0.0), axis=1, keepdims=True)


def own_kernel(frames, gain, qkv_weight, normed_out, projected_out):
    hat, _ = normalize(frames[...].astype(F32))
    normed = (hat * gain[...]).astype(BF)
    normed_out[...] = normed
    projected_out[...] = mm(normed, qkv_weight[...]).astype(BF)


def spread_heads(pair, low_lanes):
    zero = jnp.zeros_like(pair)
    return jnp.concatenate([jnp.where(low_lanes, pair, zero), jnp.where(low_lanes, zero, pair)], 0)


def main_kernel(
    device_count,
    head_size,
    frames,
    halo_one,
    halo_two,
    normed,
    projected,
    gain,
    qkv_weight,
    out_weight,
    head_gain,
    head_weight,
    frame_valid,
    targets,
    normed_all,
    grad_pairs,
    attended,
    resid_low,
    grad_resid,
    grad_normed,
    send_one,
    send_two,
    pairs,
    weights,
):
    rows, features = frames.shape
    position = lax.axis_index(EVERY)
    odd = lax.rem(position, 2) == 1
    row_one = pl.multiple_of(jnp.where(odd, 0, WIN + rows), 128)
    row_two = pl.multiple_of(jnp.where(odd, WIN + rows, 0), 128)
    scale = 1.0 / math.sqrt(head_size)
    key_count = rows + 2 * WIN

    for row, halo in ((row_one, halo_one), (row_two, halo_two)):
        hat, _ = normalize(halo[...].astype(F32))
        rim = (hat * gain[...]).astype(BF)
        normed_all[pl.ds(row, WIN), :] = rim
        pairs[pl.ds(row, WIN), :] = mm(rim, qkv_weight[:, features:]).astype(BF)
    normed_all[WIN : WIN + rows, :] = normed[...]
    pairs[WIN : WIN + rows, :] = projected[:, features:]

    query_pos = lax.broadcasted_iota(jnp.int32, (rows, key_count), 0)
    key_pos = lax.broadcasted_iota(jnp.int32, (rows, key_count), 1)
    first = jnp.where(position == 0, WIN, 0)
    last = jnp.where(position == device_count - 1, WIN + rows, key_count)
    distance = key_pos - WIN - query_pos
    allowed = (jnp.abs(distance) <= WIN) & (key_pos >= first) & (key_pos < last)
    bias = jnp.where(allowed, 0.0, -1e30).astype(F32)
    bias = jnp.concatenate([bias, bias], 0)
    low_lanes = lax.broadcasted_iota(jnp.int32, (rows, LANES), 1) < head_size
    groups = features // LANES

    for g in range(groups):
        cols = slice(g * LANES, (g + 1) * LANES)
        values = slice(features + g * LANES, features + (g + 1) * LANES)
        queries = spread_heads(projected[:, cols] * BF(scale), low_lanes)
        scores = mm_cols(queries, pairs[:, cols]) + bias
        powers = jnp.exp(scores - jnp.max(scores, axis=-1, keepdims=True))
        share = powers * (1.0 / jnp.sum(powers, axis=-1, keepdims=True))
        weights[g] = share
        mixed = mm(share.astype(BF), pairs[:, values])
        attended[:, cols] = jnp.where(low_lanes, mixed[:rows], mixed[rows:]).astype(BF)

    residual = (frames[...].astype(F32) + mm(attended[...], out_weight[...])).astype(BF)
    head_hat, head_inverse = normalize(residual.astype(F32))
    head_in = (head_hat * head_gain[...]).astype(BF)
    logits = mm(head_in, head_weight[...])
    powers = jnp.exp(logits - jnp.max(logits, axis=-1, keepdims=True))
    predicted = powers * (1.0 / jnp.sum(powers, axis=-1, keepdims=True))
    codes = lax.broadcasted_iota(jnp.int32, logits.shape, 1).astype(F32)
    one_hot = jnp.where(codes == as_column(targets[...]), 1.0, 0.0)
    grad_logits = (as_column(frame_valid[...]) * (predicted - one_hot)).astype(BF)
    grad_head = mm_cols(grad_logits, head_weight[...])
    resid = norm_back(grad_head, head_hat, head_inverse, head_gain[...])
    grad_resid[...] = resid
    low = resid.astype(BF)
    resid_low[...] = low
    grad_attended = mm_cols(low, out_weight[...]).astype(BF)

    grad_pairs[0:WIN, 0:features] = jnp.zeros((WIN, features), BF)
    grad_pairs[WIN + rows :, 0:features] = jnp.zeros((WIN, features), BF)
    for g in range(groups):
        cols = slice(g * LANES, (g + 1) * LANES)
        values = slice(features + g * LANES, features + (g + 1) * LANES)
        queries = spread_heads(projected[:, cols] * BF(scale), low_lanes)
        upstream = spread_heads(grad_attended[:, cols], low_lanes)
        share = weights[g]
        grad_weights = mm_cols(upstream, pairs[:, values])
        row_dot = jnp.sum(share * grad_weights, axis=-1, keepdims=True)
        grad_scores = (share * (grad_weights - row_dot)).astype(BF)
        mixed = mm(grad_scores, pairs[:, cols])
        grad_query = jnp.where(low_lanes, mixed[:rows], mixed[rows:]) * scale
        grad_pairs[WIN : WIN + rows, cols] = grad_query.astype(BF)
        grad_pairs[:, features + g * LANES : features + (g + 1) * LANES] = mm_rows(
            grad_scores, queries
        ).astype(BF)
        grad_pairs[:, 2 * features + g * LANES : 2 * features + (g + 1) * LANES] = mm_rows(
            share.astype(BF), upstream
        ).astype(BF)

    grad_normed[...] = mm_cols(grad_pairs[WIN : WIN + rows, :], qkv_weight[...])
    send_one[...] = mm_cols(
        grad_pairs[pl.ds(row_one, WIN), features:], qkv_weight[:, features:]
    ).astype(BF)
    send_two[...] = mm_cols(
        grad_pairs[pl.ds(row_two, WIN), features:], qkv_weight[:, features:]
    ).astype(BF)


def input_kernel(frames, gain, grad_resid, grad_normed, from_one, from_two, grad_input):
    hat, inverse = normalize(frames[...].astype(F32))
    total = grad_normed[...] + from_one[...].astype(F32) + from_two[...].astype(F32)
    grad_input[...] = grad_resid[...] + norm_back(total, hat, inverse, gain[...])


def half_kernel(sizes, other, normed_all, grad_pairs, attended, resid_low, share):
    inner_count, outer_count = sizes
    features = normed_all.shape[1]
    core = lax.rem(lax.axis_index("inner"), 2)
    if other:
        core = 1 - core
    wide = grad_pairs.shape[1] // inner_count
    narrow = features // inner_count
    tall = features // outer_count
    for x in range(inner_count // 2):
        block = 2 * x + core
        left = mm_rows(
            normed_all[...], grad_pairs[:, pl.ds(pl.multiple_of(block * wide, LANES), wide)]
        ).astype(share.dtype)
        right = mm_rows(
            attended[...], resid_low[:, pl.ds(pl.multiple_of(block * narrow, LANES), narrow)]
        ).astype(share.dtype)
        for o in range(outer_count):
            z, y = divmod(o, 2)
            row = ((x * 2 + y) * (outer_count // 2) + z) * tall
            share[row : row + tall, :wide] = left[o * tall : (o + 1) * tall]
            share[row : row + tall, wide:] = right[o * tall : (o + 1) * tall]


def square_kernel(sizes, kept, received, *outs):
    inner_count, _ = sizes
    x = lax.axis_index("inner") // 2
    y = lax.rem(lax.axis_index("outer"), 2)
    parts = inner_count
    height = kept.shape[0] // parts
    mine = x * 2 + y
    for k, out in enumerate(outs):
        row = pl.multiple_of((mine ^ k) * height, height)
        total = kept[pl.ds(row, height), :] + received[pl.ds(row, height), :].astype(F32)
        out[...] = total.astype(out.dtype)


def line_kernel(sizes, kept, *refs):
    inner_count, outer_count = sizes
    received, outs = refs[: inner_count - 1], refs[inner_count - 1 :]
    parts = outer_count // 2
    height = kept.shape[0] // parts
    mine = lax.axis_index("outer") // 2
    for k, out in enumerate(outs):
        rows = pl.ds(pl.multiple_of((mine ^ k) * height, height), height)
        total = kept[rows, :]
        for other in received:
            total = total + other[rows, :].astype(F32)
        out[...] = total.astype(out.dtype)


def last_kernel(kept, *refs):
    received, (qkv_out, out_out) = refs[:-2], refs[-2:]
    total = kept[...]
    for other in received:
        total = total + other[...].astype(F32)
    wide = qkv_out.shape[1]
    qkv_out[...] = total[:, :wide]
    out_out[...] = total[:, wide:]


def full_kernel(normed_all, grad_pairs, attended, resid_low, qkv_out, out_out):
    qkv_out[...] = mm_rows(normed_all[...], grad_pairs[...])
    out_out[...] = mm_rows(attended[...], resid_low[...])


def call(kernel, outs, *args, name, scratch=(), final=False, limit=24):
    if final:
        shapes = [jax.ShapeDtypeStruct(shape, dtype) for shape, dtype in outs]
    else:
        shapes = [pltpu.VMEM(shape, dtype) for shape, dtype in outs]
    args = [pltpu.with_memory_space_constraint(arg, pltpu.VMEM) for arg in args]
    spec = pl.BlockSpec(memory_space=pltpu.VMEM)
    return pl.pallas_call(
        kernel,
        out_shape=shapes,
        in_specs=[spec] * len(args),
        out_specs=[spec] * len(shapes),
        scratch_shapes=list(scratch),
        compiler_params=pltpu.CompilerParams(vmem_limit_bytes=limit << 20),
        name=name,
    )(*args)


def grid_swap(sizes, inner_bits, outer_bits):
    inner_count, outer_count = sizes
    return [
        (i * outer_count + o, (i ^ inner_bits) * outer_count + (o ^ outer_bits))
        for i in range(inner_count)
        for o in range(outer_count)
    ]


def swap(value, sizes, inner_bits, outer_bits):
    return lax.ppermute(value, EVERY, grid_swap(sizes, inner_bits, outer_bits))


def neighbour_swaps(device_count):
    near = [(i, i ^ 1) for i in range(device_count // 2 * 2)]
    far = [(i, i + 1) for i in range(1, device_count - 1, 2)]
    return near, far + [(j, i) for i, j in far]


def power_of_two(count):
    return count > 1 and count & (count - 1) == 0


def per_device(
    sizes,
    frames,
    attention_gain,
    qkv_weight,
    out_weight,
    head_gain,
    head_weight,
    frame_valid,
    targets,
):
    inner_count, outer_count = sizes
    device_count = inner_count * outer_count
    rows, features = frames.shape
    columns = qkv_weight.shape[1]
    key_count = rows + 2 * WIN
    near, far = neighbour_swaps(device_count)
    halo_two = lax.ppermute(frames, EVERY, far)
    halo_one = lax.ppermute(frames, EVERY, near)
    gain = attention_gain.reshape(1, features)
    normed, projected = call(
        own_kernel,
        [((rows, features), BF), ((rows, columns), BF)],
        frames,
        gain,
        qkv_weight,
        name="own",
    )
    (
        normed_all,
        grad_pairs,
        attended,
        resid_low,
        grad_resid,
        grad_normed,
        send_one,
        send_two,
    ) = call(
        functools.partial(main_kernel, device_count, features // HEADS),
        [
            ((key_count, features), BF),
            ((key_count, columns), BF),
            ((rows, features), BF),
            ((rows, features), BF),
            ((rows, features), F32),
            ((rows, features), F32),
            ((WIN, features), BF),
            ((WIN, features), BF),
        ],
        frames,
        halo_one,
        halo_two,
        normed,
        projected,
        gain,
        qkv_weight,
        out_weight,
        head_gain.reshape(1, features),
        head_weight,
        frame_valid.reshape(1, rows),
        targets.reshape(1, rows),
        name="main",
        scratch=[
            pltpu.VMEM((key_count, 2 * features), BF),
            pltpu.VMEM((features // LANES, 2 * rows, key_count), F32),
        ],
    )
    from_two = lax.ppermute(send_two, EVERY, far)
    from_one = lax.ppermute(send_one, EVERY, near)
    (grad_input,) = call(
        input_kernel,
        [((rows, features), F32)],
        frames,
        gain,
        grad_resid,
        grad_normed,
        from_one,
        from_two,
        name="input",
        final=True,
    )
    terms = (normed_all, grad_pairs, attended, resid_low)
    wide, narrow = columns // inner_count, features // inner_count
    tall = features // outer_count
    tiled = wide % LANES == 0 and narrow % LANES == 0 and tall % 16 == 0
    if tiled and power_of_two(inner_count) and power_of_two(outer_count):
        half = inner_count // 2 * features
        width = wide + narrow
        (away,) = call(
            functools.partial(half_kernel, sizes, True), [((half, width), BF)], *terms, name="away"
        )
        received = swap(away, sizes, 1, 0)
        (home,) = call(
            functools.partial(half_kernel, sizes, False), [((half, width), F32)], *terms, name="home"
        )
        height = half // inner_count
        kept, *sends = call(
            functools.partial(square_kernel, sizes),
            [((height, width), F32)] + [((height, width), BF)] * (inner_count - 1),
            home,
            received,
            name="square",
        )
        got = [
            swap(send, sizes, (k >> 1) << 1, k & 1)
            for k, send in reversed(list(enumerate(sends, 1)))
        ]
        parts = outer_count // 2
        kept, *sends = call(
            functools.partial(line_kernel, sizes),
            [((tall, width), F32)] + [((tall, width), BF)] * (parts - 1),
            kept,
            *got,
            name="line",
        )
        got = [swap(send, sizes, 0, k << 1) for k, send in reversed(list(enumerate(sends, 1)))]
        grad_qkv, grad_out = call(
            last_kernel, [((tall, wide), F32), ((tall, narrow), F32)], kept, *got, name="last", final=True
        )
        return grad_input, grad_qkv, grad_out
    proj_term, output_term = call(
        full_kernel, [((features, columns), F32), ((features, features), F32)], *terms, name="full", final=True
    )
    proj_term = proj_term.reshape(features, inner_count, wide)
    output_term = output_term.reshape(features, inner_count, narrow)
    joined = jnp.concatenate([proj_term, output_term], 2).reshape(features, -1)
    shares = lax.psum_scatter(joined, "inner", scatter_dimension=1, tiled=True)
    shares = lax.psum_scatter(shares, "outer", scatter_dimension=0, tiled=True)
    return grad_input, shares[:, :wide], shares[:, wide:]


def solution(mesh):
    sizes = (mesh.shape["inner"], mesh.shape["outer"])
    spread = P(EVERY)
    return jax.shard_map(
        functools.partial(per_device, sizes),
        mesh=mesh,
        in_specs=(P(EVERY, None), P(), P(), P(), P(), P(), spread, spread),
        out_specs=(P(EVERY, None), P("outer", "inner"), P("outer", "inner")),
        check_vma=False,
    )
```
